1024 devices in a mesh: ep: 32 (over y, x, core), tp: 32 (over z).
Axes of the slice: x: 4, y: 4, z: 32, core: 2. Of those that a mesh axis runs over, the one named last changes fastest.
Arguments:
- attn: bfloat16 [2048, 4096], P('ep', 'tp'), may hold values from -6 to 6
- norm_gain: float32 [4096], replicated, may hold values from 0.5 to 1.5
- w_gate: bfloat16 [32, 1792, 4096], P('ep', 'tp'), may hold values from -0.09375 to 0.09375
- w_up: bfloat16 [32, 1792, 4096], P('ep', 'tp'), may hold values from -0.09375 to 0.09375
- w_down: bfloat16 [32, 1792, 4096], P('ep', 'tp'), may hold values from -0.0625 to 0.0625
- expert_ids: int32 [2048, 2], P('ep'), may hold values from 0 to 7, all different within a row; in each aligned block of 64 rows (0 to 63, 64 to 127, ...) at most 24 rows name the same one
- gate_fix: int32 [2048, 2], P('ep'), may hold values from 1 to 65535, as said below
Outputs:
- moe_out: bfloat16 [2048, 4096], P('ep', 'tp')
The draws below stay inside these ranges and needn't reach their ends.
Inputs may be any that keep to these rules, and one draw needn't show every extreme that they name: `expert_ids`: among the tokens of one ep index (64 rows), no expert is named by more than 24 routes, a bound that some block reaches; a row names 2 different experts. `gate_fix`: the 2 entries of a row sum to 65536.
All inputs are finite; a program needn't handle non-finite values.
Results may differ from the reference program's by a relative error of at most 0.0065.
Values may be sent and summed in bfloat16 or wider, within the bound.
No kernel may reach another device: no remote copies, remote signals or barrier semaphores. Data moves between devices by JAX's collectives and lax.ppermute only.
A program may use at most 32 MiB of HBM per device.

```python
import math
import jax
import jax.numpy as jnp
import numpy as np
from jax import lax

D = 4096
EXPERTS = 8
TOP = 2
EXPERT_FF = 7168
ROW_TOK = 64
SLICES = 4
HID_COPY = 1792
CAP = 24
TOKENS = 2048
N_EP = 32


def draw_gate_fix(key, part):
    first = jax.random.randint(key, (TOKENS, 1), 1, 65536, dtype=jnp.int32)
    return jnp.concatenate([first, 65536 - first], axis=1)


def block_levels(own_key, extent, pieces, low, largest):
    def one(dim, shards_of):
        heights = jax.random.uniform(jax.random.fold_in(jax.random.fold_in(own_key, 6), dim), (shards_of,), jnp.float32, low / len(pieces), largest / len(pieces))
        return jnp.repeat(jnp.exp(heights), extent[dim] // shards_of).reshape((-1,) + (1,) * (len(extent) - dim - 1))

    factor_of = one(*pieces[0])
    for cut in pieces[1:]:
        factor_of = factor_of * one(*cut)
    return factor_of


def deal_out(rng, own, number, rows, amount, top, limit, slope):
    sequence = jax.random.permutation(rng, amount)
    crowded, common = load_shares(amount, rows * top, limit, slope, True), load_shares(amount, rows * top, limit, slope, False)
    places = jnp.arange(amount)

    def named(sizes, rotation):
        used = int((sizes > 0).sum())
        fixed = max(1, used // 4)
        passed = fixed + (places - fixed + rotation * (used - fixed)) % max(1, amount - fixed)
        return jnp.zeros((amount,), jnp.int32).at[sequence[jnp.where(places < fixed, places, passed)]].set(jnp.asarray(sizes, jnp.int32))

    sizes = jnp.where(number % 4 == 0, named(crowded, number // 4), named(common, number - number // 4 - 1))
    mixed = jax.random.permutation(jax.random.fold_in(own, 3), amount)
    giver, taker = mixed[0:amount // 2 * 2:2], mixed[1:amount // 2 * 2:2]
    room = jnp.minimum(sizes[giver] - 1, limit - sizes[taker]) // 2
    room = jnp.where((giver == sequence[0]) | (taker == sequence[0]) | (sizes[taker] == 0), 0, jnp.maximum(room, 0))
    passed = jax.random.randint(jax.random.fold_in(own, 4), (amount // 2,), 0, 1 << 20) % (room + 1)
    sizes = sizes.at[giver].add(-passed).at[taker].add(passed)
    members = jnp.searchsorted(jnp.cumsum(sizes), jnp.arange(rows * top), side="right").astype(jnp.int32)
    table = members.reshape(top, rows).T
    table = table[jax.random.permutation(jax.random.fold_in(own, 1), rows)]
    rotation = jax.random.randint(jax.random.fold_in(own, 2), (rows, 1), 0, top)
    return jnp.take_along_axis(table, (jnp.arange(top)[None, :] + rotation) % top, axis=1)


def load_shares(amount, total, most, skew, full):
    weights = [(1 << 20) // math.isqrt(grade ** skew) + 1 for grade in range(1, amount + 1)]
    largest = most if full else min(most, max(-(-total // amount), total * weights[0] // sum(weights)))
    least = 1 if total - largest >= amount - 1 else 0
    holding, surplus = [largest] + [least] * (amount - 1), total - largest - least * (amount - 1)
    while surplus > 0:
        candidates = [i for i in range(1, amount) if holding[i] < largest] or [i for i in range(1, amount) if holding[i] < most]
        pool, remaining = sum([weights[i] for i in candidates]), surplus
        for i in candidates:
            addition = min(most - holding[i], max(1, remaining * weights[i] // pool), surplus)
            holding[i] = holding[i] + addition
            surplus = surplus - addition
    return np.array(holding)


def bell_draw(stream_key, dims, deviation, bound, split=(), kind=jnp.bfloat16):
    gain = block_levels(stream_key, dims, split, -0.22, 0.18) if split else 1.0
    result = jax.random.normal(stream_key, dims, jnp.float32) * deviation * gain
    return jnp.minimum(jnp.maximum(result, -bound), bound).astype(kind)


def setup_inputs(seed: int = 0) -> dict:
    arg_keys = jax.random.split(jax.random.key(seed), 8)
    attn = bell_draw(arg_keys[0], (TOKENS, D), 1.0, 6.0, ((0, 32), (1, 32)))
    norm_gain = jnp.clip(1.0 + 0.1 * jax.random.normal(arg_keys[1], (D,), jnp.float32), 0.5, 1.5)
    w_gate = bell_draw(arg_keys[2], (N_EP, HID_COPY, D), D ** -0.5, 0.09375, ((0, 32), (1, 32)))
    w_up = bell_draw(arg_keys[3], (N_EP, HID_COPY, D), D ** -0.5, 0.09375, ((0, 32), (1, 32)))
    w_down = bell_draw(arg_keys[4], (N_EP, HID_COPY, D), EXPERT_FF ** -0.5, 0.0625, ((0, 32), (1, 32)))
    expert_ids_keys = jax.random.split(jax.random.fold_in(arg_keys[5], 1), TOKENS // ROW_TOK)
    expert_ids_turns = jax.random.permutation(jax.random.fold_in(arg_keys[5], 3), TOKENS // ROW_TOK)
    expert_ids = jax.vmap(lambda own, number: deal_out(jax.random.fold_in(arg_keys[5], 2), own, number, ROW_TOK, EXPERTS, TOP, CAP, 2))(expert_ids_keys, expert_ids_turns).reshape((TOKENS, TOP))
    gate_fix = draw_gate_fix(jax.random.fold_in(arg_keys[7], 71), 0)
    return {"attn": attn, "norm_gain": norm_gain, "w_gate": w_gate, "w_up": w_up, "w_down": w_down, "expert_ids": expert_ids, "gate_fix": gate_fix}


def route_ordinal(route_ids):
    flat_ids = route_ids.reshape(-1)
    onehot = (flat_ids[:, None] == jnp.arange(EXPERTS, dtype=jnp.int32)[None, :]).astype(jnp.int32)
    before = jnp.cumsum(onehot, axis=0) - onehot
    return lax.optimization_barrier(jnp.sum(before * onehot, axis=1)).astype(jnp.int32)

def contract_last(left, right):
    return lax.dot_general(left, right, (((1,), (1,)), ((), ())), preferred_element_type=jnp.float32)

def reference(attn, norm_gain, w_gate, w_up, w_down, expert_ids, gate_fix):
    values = attn.astype(jnp.float32)
    inverse_rms = lax.rsqrt(lax.optimization_barrier(jnp.mean(values * values, axis=-1, keepdims=True)) + 1e-05)
    normed = (values * inverse_rms * norm_gain).astype(jnp.bfloat16)
    block_ids = expert_ids.reshape(N_EP, ROW_TOK * TOP)
    ordinal = jax.vmap(route_ordinal)(block_ids)
    route_tok = jnp.arange(ROW_TOK * TOP, dtype=jnp.int32) // TOP
    token_index = jnp.arange(N_EP, dtype=jnp.int32)[:, None] * ROW_TOK + route_tok[None, :]
    source_index = jnp.broadcast_to(jnp.arange(N_EP, dtype=jnp.int32)[:, None], block_ids.shape)
    buffers = jnp.zeros((N_EP, N_EP, CAP, D), jnp.bfloat16)
    routed_rows = normed[token_index]
    for slice_index in range(SLICES):
        owner = block_ids * SLICES + slice_index
        buffers = buffers.at[source_index, owner, ordinal].set(routed_rows)

    def run_owner(owner_index):
        slot_rows = buffers[:, owner_index].reshape(N_EP * CAP, D)
        gate_act = contract_last(slot_rows, w_gate[owner_index])
        up_act = contract_last(slot_rows, w_up[owner_index])
        hidden_act = (jax.nn.silu(gate_act) * up_act).astype(jnp.bfloat16)
        expert_out = jnp.dot(hidden_act, w_down[owner_index], preferred_element_type=jnp.float32)
        return expert_out.reshape(N_EP, CAP, D)
    results = lax.map(run_owner, jnp.arange(N_EP, dtype=jnp.int32))
    picked = jnp.zeros((N_EP, ROW_TOK * TOP, D), jnp.float32)
    for slice_index in range(SLICES):
        owner = block_ids * SLICES + slice_index
        picked = picked + results[owner, source_index, ordinal]
    route_weight = gate_fix.astype(jnp.float32).reshape(N_EP, ROW_TOK * TOP) / 65536.0
    weighted = (picked * route_weight[:, :, None]).reshape(N_EP, ROW_TOK, TOP, D)
    return lax.optimization_barrier(jnp.sum(weighted, axis=2)).reshape(TOKENS, D).astype(jnp.bfloat16)
```

```python
import jax
import jax.numpy as jnp
from jax import lax
from jax.sharding import Mesh
from jax.sharding import PartitionSpec as P

EXPERTS = 8
EP = ("eh", "xl", "core")
TP = ("zh", "zl")
QUAD = ("xl", "core")
SWAP = [(0, 1), (1, 0)]


def route_ordinal(route_ids):
    flat_ids = route_ids.reshape(-1)
    onehot = (flat_ids[:, None] == jnp.arange(EXPERTS, dtype=jnp.int32)[None, :]).astype(jnp.float32)
    count = flat_ids.shape[0]
    earlier = (jnp.arange(count)[:, None] > jnp.arange(count)[None, :]).astype(jnp.float32)
    before = jnp.dot(earlier, onehot, preferred_element_type=jnp.float32)
    return jnp.sum(before * onehot, axis=1).astype(jnp.int32)


def contract_last(left, right):
    return lax.dot_general(
        left, right, (((1,), (1,)), ((), ())), preferred_element_type=jnp.float32
    )


def pair_up(mine, other, position):
    low = jnp.where(position == 0, mine, other)
    high = jnp.where(position == 0, other, mine)
    return jnp.stack([low, high])


def body(attn, norm_gain, w_gate, w_up, w_down, expert_ids, gate_fix):
    owners = lax.axis_size(EP)
    n_zh, n_zl = lax.axis_size("zh"), lax.axis_size("zl")
    xl, core = lax.axis_index("xl"), lax.axis_index("core")
    row_tok, cols = attn.shape
    width = norm_gain.shape[0]
    top_count = expert_ids.shape[1]
    cap = 3 * row_tok // 8
    slices = owners // EXPERTS
    part = width // slices
    key_count = EXPERTS * cap
    hid = w_gate.shape[1]

    stacked = jnp.concatenate([w_gate, w_up, w_down], axis=0)
    half = width // 2
    keep_x = lax.dynamic_slice_in_dim(stacked, xl * half, half, axis=2)
    send_x = lax.dynamic_slice_in_dim(stacked, (1 - xl) * half, half, axis=2)
    got_x = lax.ppermute(send_x, "xl", SWAP)

    rows = lax.all_gather(attn, "zl", axis=1, tiled=True)
    rows = lax.all_gather(rows, "zh", axis=1, tiled=True)
    rows, got_x = lax.optimization_barrier((rows, got_x))

    pair_x = pair_up(keep_x, got_x, xl)
    keep_c = lax.dynamic_slice_in_dim(pair_x, core * part, part, axis=3)
    send_c = lax.dynamic_slice_in_dim(pair_x, (1 - core) * part, part, axis=3)
    got_c = lax.ppermute(send_c, "core", SWAP)

    ordinal = route_ordinal(expert_ids)
    target = expert_ids.reshape(-1) * cap + ordinal
    hits = (target[:, None] == jnp.arange(key_count, dtype=jnp.int32)[None, :]).astype(jnp.float32)
    hits = hits.reshape(row_tok, top_count, key_count)
    pick_rows = jnp.sum(hits, axis=1).T.astype(jnp.bfloat16)
    high = (gate_fix // 256).astype(jnp.float32)
    low = (gate_fix % 256).astype(jnp.float32)
    combine_map = jnp.concatenate(
        [jnp.sum(hits * high[:, :, None], axis=1), jnp.sum(hits * low[:, :, None], axis=1)], axis=0
    ).astype(jnp.bfloat16)

    values = rows.astype(jnp.float32)
    inverse_rms = lax.rsqrt(jnp.mean(values * values, axis=-1, keepdims=True) + 1e-05)
    normed = (values * inverse_rms * norm_gain).astype(jnp.bfloat16)
    by_expert = jnp.dot(pick_rows, normed, preferred_element_type=jnp.float32).astype(jnp.bfloat16)
    outgoing = by_expert.reshape(EXPERTS, cap, slices, part).transpose(0, 2, 1, 3)
    incoming = lax.all_to_all(outgoing.reshape(owners, cap, part), EP, split_axis=0, concat_axis=0, tiled=True)
    incoming, got_c = lax.optimization_barrier((incoming, got_c))
    slot_rows = incoming.reshape(owners * cap, part)

    quad = pair_up(keep_c, got_c, core).transpose(2, 1, 0, 3, 4)
    hidden_quad = slices * hid
    quad = quad.reshape(3, hidden_quad, part)
    gate_part = contract_last(slot_rows, quad[0]).astype(jnp.bfloat16)
    up_part = contract_last(slot_rows, quad[1]).astype(jnp.bfloat16)
    group = owners * cap // slices
    parts = jnp.stack(
        [gate_part.reshape(slices, group, hidden_quad), up_part.reshape(slices, group, hidden_quad)], axis=1
    )
    parts = lax.all_to_all(parts, QUAD, split_axis=0, concat_axis=0, tiled=True)
    sums = jnp.sum(parts.astype(jnp.float32), axis=0)
    hidden_act = (jax.nn.silu(sums[0]) * sums[1]).astype(jnp.bfloat16)
    spread = jnp.broadcast_to(hidden_act[None], (slices,) + hidden_act.shape)
    hidden_all = lax.all_to_all(spread, QUAD, split_axis=0, concat_axis=0, tiled=True)
    slice_out = jnp.dot(hidden_all.reshape(owners * cap, hidden_quad), quad[2], preferred_element_type=jnp.float32)
    slice_out = slice_out.astype(jnp.bfloat16).reshape(owners, cap, part)
    returned = lax.all_to_all(slice_out, EP, split_axis=0, concat_axis=0, tiled=True)

    returned = returned.reshape(EXPERTS, slices, cap, part).transpose(0, 2, 1, 3).reshape(key_count, width)
    both = jnp.dot(combine_map, returned, preferred_element_type=jnp.float32)
    combined = both[:row_tok] * (1.0 / 256.0) + both[row_tok:] * (1.0 / 65536.0)
    pieces = combined.astype(jnp.bfloat16).reshape(row_tok, n_zh, n_zl, cols).transpose(2, 1, 0, 3)
    pieces = lax.all_to_all(pieces, "zl", split_axis=0, concat_axis=0, tiled=True)
    pieces = jnp.sum(pieces.astype(jnp.float32), axis=0).astype(jnp.bfloat16)
    pieces = lax.all_to_all(pieces, "zh", split_axis=0, concat_axis=0, tiled=True)
    return jnp.sum(pieces.astype(jnp.float32), axis=0).astype(jnp.bfloat16)


def solution(mesh):
    n_ep, n_tp = mesh.devices.shape
    near = 4 if n_tp % 4 == 0 else 1
    fine = Mesh(
        mesh.devices.reshape(n_ep // 4, 2, 2, n_tp // near, near), ("eh", "xl", "core", "zh", "zl")
    )
    in_specs = (
        P(EP, TP),
        P(),
        P(EP, TP, None),
        P(EP, TP, None),
        P(EP, TP, None),
        P(EP, None),
        P(EP, None),
    )
    return jax.shard_map(body, mesh=fine, in_specs=in_specs, out_specs=P(EP, TP), check_vma=False)
```

```python
import jax
import jax.numpy as jnp
from jax import lax
from jax.experimental import pallas as pl
from jax.experimental.pallas import tpu as pltpu
from jax.sharding import Mesh
from jax.sharding import PartitionSpec as P

EXPERTS = 8
TP = ("zh", "zl")
NEAR = 4
LANES = 128
VMEM = pl.BlockSpec(memory_space=pltpu.VMEM)
SMEM = pl.BlockSpec(memory_space=pltpu.SMEM)


def route_ordinal(route_ids):
    flat_ids = route_ids.reshape(-1)
    onehot = (flat_ids[:, None] == jnp.arange(EXPERTS, dtype=jnp.int32)[None, :]).astype(jnp.float32)
    count = flat_ids.shape[0]
    earlier = (jnp.arange(count)[:, None] > jnp.arange(count)[None, :]).astype(jnp.float32)
    before = jnp.dot(earlier, onehot, preferred_element_type=jnp.float32)
    return jnp.sum(before * onehot, axis=1).astype(jnp.int32)


def deal_kernel(place, gain, gate, up, down, own_gain, *outs):
    blocks = gate.shape[1] // (NEAR * LANES)
    for i in range(blocks):
        to = slice(i * LANES, (i + 1) * LANES)
        for r, out in enumerate(outs):
            quarter = lax.rem(place[0] + r, NEAR)
            at = pl.ds(pl.multiple_of((quarter + NEAR * i) * LANES, LANES), LANES)
            for k, weight in enumerate((gate, up, down)):
                out[k, :, to] = weight[:, at]
            if r == 0:
                own_gain[:, to] = gain[:, at]


def gather_kernel(place, gain, *refs):
    pieces, (high, low, down) = refs[:NEAR], refs[NEAR:]
    for r, piece in enumerate(pieces):
        source = lax.rem(place[0] - r + NEAR, NEAR)
        for k in range(2):
            scaled = piece[k].astype(jnp.float32) * gain[...]
            rounded = scaled.astype(jnp.bfloat16)
            high[k, source] = rounded
            low[k, source] = (scaled - rounded.astype(jnp.float32)).astype(jnp.bfloat16)
        down[source] = piece[2]


def act_kernel(rows, high, low, out):
    x = rows[...]
    dims = (((1,), (1,)), ((), ()))
    acts = lax.dot_general(x, high[...], dims, preferred_element_type=jnp.float32)
    acts = acts + lax.dot_general(x, low[...], dims, preferred_element_type=jnp.float32)
    values = x.astype(jnp.float32)
    squares = jnp.sum(values * values, axis=1, keepdims=True)
    rounded = squares.astype(jnp.bfloat16).astype(jnp.float32)
    tail = out.shape[1] - acts.shape[1]
    column = lax.broadcasted_iota(jnp.int32, (x.shape[0], tail), 1)
    extra = jnp.where(column == 0, rounded, jnp.where(column == 1, squares - rounded, 0.0))
    out[:, : acts.shape[1]] = acts.astype(jnp.bfloat16)
    out[:, acts.shape[1] :] = extra.astype(jnp.bfloat16)


def body(attn, norm_gain, w_gate, w_up, w_down, expert_ids, gate_fix):
    owners = lax.axis_size("ep")
    n_zh = lax.axis_size("zh")
    place = lax.axis_index("zl").reshape(1)
    row_tok, cols = attn.shape
    width = norm_gain.shape[0]
    top_count = expert_ids.shape[1]
    cap = 3 * row_tok // 8
    slices = owners // EXPERTS
    part = width // NEAR
    hid = w_gate.shape[1]
    slots = owners * cap
    bf16, f32 = jnp.bfloat16, jnp.float32

    copies = jnp.broadcast_to(attn[None], (n_zh, row_tok, cols))
    rows = lax.all_to_all(copies, "zh", split_axis=0, concat_axis=0, tiled=True)

    piece_type = jax.ShapeDtypeStruct((3, hid, part), bf16)
    own_gain, *pieces = pl.pallas_call(
        deal_kernel,
        in_specs=[SMEM] + [VMEM] * 4,
        out_specs=[VMEM] * (1 + NEAR),
        out_shape=[jax.ShapeDtypeStruct((1, part), f32)] + [piece_type] * NEAR,
        name="deal",
    )(place, norm_gain.reshape(1, width), w_gate[0], w_up[0], w_down[0])
    for r in range(1, NEAR):
        pieces[r] = lax.ppermute(pieces[r], "zl", [(i, (i + r) % NEAR) for i in range(NEAR)])

    ordinal = route_ordinal(expert_ids)
    target = (expert_ids.reshape(-1) * slices) * cap + ordinal
    key = jnp.arange(slots, dtype=jnp.int32)
    key = key - ((key // cap) % slices) * cap
    hits = (target[:, None] == key[None, :]).astype(f32).reshape(row_tok, top_count, slots)
    pick_rows = jnp.sum(hits, axis=1).astype(bf16)
    high = (gate_fix // 256).astype(f32)
    low = (gate_fix % 256).astype(f32)
    combine_map = jnp.concatenate(
        [jnp.sum(hits * high[:, :, None], axis=1), jnp.sum(hits * low[:, :, None], axis=1)], axis=0
    ).astype(bf16)

    rows = rows.transpose(1, 0, 2).reshape(row_tok, part)
    outgoing = lax.dot_general(pick_rows, rows, (((0,), (0,)), ((), ())), preferred_element_type=f32)
    outgoing = outgoing.astype(bf16).reshape(owners, cap, part)
    incoming = lax.all_to_all(outgoing, "ep", split_axis=0, concat_axis=0, tiled=True)

    four = NEAR * hid
    gate_up_high, gate_up_low, down = pl.pallas_call(
        gather_kernel,
        in_specs=[SMEM] + [VMEM] * (1 + NEAR),
        out_specs=[VMEM] * 3,
        out_shape=[jax.ShapeDtypeStruct((2, NEAR, hid, part), bf16)] * 2
        + [jax.ShapeDtypeStruct((NEAR, hid, part), bf16)],
        name="gather",
    )(place, own_gain, *pieces)

    group = slots // NEAR
    lanes = -(-(2 * four + 2) // LANES) * LANES
    acts = pl.pallas_call(
        act_kernel,
        grid=(NEAR,),
        in_specs=[
            pl.BlockSpec((group, part), lambda g: (g, 0)),
            pl.BlockSpec((2 * four, part), lambda g: (0, 0)),
            pl.BlockSpec((2 * four, part), lambda g: (0, 0)),
        ],
        out_specs=pl.BlockSpec((group, lanes), lambda g: (g, 0)),
        out_shape=jax.ShapeDtypeStruct((slots, lanes), bf16),
        name="acts",
    )(incoming.reshape(slots, part), gate_up_high.reshape(2 * four, part), gate_up_low.reshape(2 * four, part))
    acts = lax.all_to_all(acts.reshape(NEAR, group, lanes), "zl", split_axis=0, concat_axis=0, tiled=True)
    sums = jnp.sum(acts.astype(f32), axis=0)
    squares = sums[:, 2 * four : 2 * four + 1] + sums[:, 2 * four + 1 : 2 * four + 2]
    inverse_rms = lax.rsqrt(squares / width + 1e-05)
    gate_act = sums[:, :four] * inverse_rms
    up_act = sums[:, four : 2 * four] * inverse_rms
    hidden_act = (jax.nn.silu(gate_act) * up_act).astype(bf16)
    spread = jnp.broadcast_to(hidden_act[None], (NEAR,) + hidden_act.shape)
    hidden_all = lax.all_to_all(spread, "zl", split_axis=0, concat_axis=0, tiled=True)

    slice_out = jnp.dot(hidden_all.reshape(slots, four), down.reshape(four, part), preferred_element_type=f32)
    slice_out = slice_out.astype(bf16).reshape(owners, cap, part)
    returned = lax.all_to_all(slice_out, "ep", split_axis=0, concat_axis=0, tiled=True)

    both = jnp.dot(combine_map, returned.reshape(slots, part), preferred_element_type=f32)
    combined = both[:row_tok] * (1.0 / 256.0) + both[row_tok:] * (1.0 / 65536.0)
    shares = combined.astype(bf16).reshape(row_tok, n_zh, cols).transpose(1, 0, 2)
    shares = lax.all_to_all(shares, "zh", split_axis=0, concat_axis=0, tiled=True)
    return jnp.sum(shares.astype(f32), axis=0).astype(bf16)


def solution(mesh):
    n_ep, n_tp = mesh.devices.shape
    fine = Mesh(mesh.devices.reshape(n_ep, n_tp // NEAR, NEAR), ("ep", "zh", "zl"))
    in_specs = (
        P("ep", TP),
        P(),
        P("ep", TP, None),
        P("ep", TP, None),
        P("ep", TP, None),
        P("ep", None),
        P("ep", None),
    )
    return jax.shard_map(body, mesh=fine, in_specs=in_specs, out_specs=P("ep", TP), check_vma=False)
```

```python
import jax
import jax.numpy as jnp
from jax import lax
from jax.experimental import pallas as pl
from jax.experimental.pallas import tpu as pltpu
from jax.sharding import Mesh
from jax.sharding import PartitionSpec as P

EXPERTS = 8
EP = ("eh", "xl", "core")
TP = ("zh", "zl")
QUAD = ("core", "zl")
NEAR = 4
LANES = 128
VMEM = pl.BlockSpec(memory_space=pltpu.VMEM)
SMEM = pl.BlockSpec(memory_space=pltpu.SMEM)


def route_ordinal(route_ids):
    flat_ids = route_ids.reshape(-1)
    onehot = (flat_ids[:, None] == jnp.arange(EXPERTS, dtype=jnp.int32)[None, :]).astype(jnp.float32)
    count = flat_ids.shape[0]
    earlier = (jnp.arange(count)[:, None] > jnp.arange(count)[None, :]).astype(jnp.float32)
    before = jnp.dot(earlier, onehot, preferred_element_type=jnp.float32)
    return jnp.sum(before * onehot, axis=1).astype(jnp.int32)


def deal_kernel(place, gain, gate, up, down, own_gain, *outs):
    blocks = gate.shape[1] // (NEAR * LANES)
    for r, out in enumerate(outs):
        core = lax.rem(place[0] + r // 2, 2)
        zl = lax.rem(place[1] + r % 2, 2)
        for i in range(blocks):
            to = slice(i * LANES, (i + 1) * LANES)
            block = (core * blocks + i) * 2 + zl
            at = pl.ds(pl.multiple_of(block * LANES, LANES), LANES)
            for k, weight in enumerate((gate, up, down)):
                out[k, :, to] = weight[:, at]
            if r == 0:
                own_gain[:, to] = gain[:, at]


def gather_kernel(place, gain, *refs):
    pieces, (high, low, down) = refs[:NEAR], refs[NEAR:]
    for r, piece in enumerate(pieces):
        source = 2 * lax.rem(place[0] + r // 2, 2) + lax.rem(place[1] + r % 2, 2)
        for k in range(2):
            scaled = piece[k].astype(jnp.float32) * gain[...]
            rounded = scaled.astype(jnp.bfloat16)
            high[k, source] = rounded
            low[k, source] = (scaled - rounded.astype(jnp.float32)).astype(jnp.bfloat16)
        down[source] = piece[2]


def act_kernel(rows, high, low, out):
    x = rows[...]
    dims = (((1,), (1,)), ((), ()))
    acts = lax.dot_general(x, high[...], dims, preferred_element_type=jnp.float32)
    acts = acts + lax.dot_general(x, low[...], dims, preferred_element_type=jnp.float32)
    values = x.astype(jnp.float32)
    squares = jnp.sum(values * values, axis=1, keepdims=True)
    rounded = squares.astype(jnp.bfloat16).astype(jnp.float32)
    tail = out.shape[1] - acts.shape[1]
    column = lax.broadcasted_iota(jnp.int32, (x.shape[0], tail), 1)
    extra = jnp.where(column == 0, rounded, jnp.where(column == 1, squares - rounded, 0.0))
    out[:, : acts.shape[1]] = acts.astype(jnp.bfloat16)
    out[:, acts.shape[1] :] = extra.astype(jnp.bfloat16)


def body(attn, norm_gain, w_gate, w_up, w_down, expert_ids, gate_fix):
    owners = lax.axis_size(EP)
    n_zh = lax.axis_size("zh")
    place = jnp.stack([lax.axis_index("core"), lax.axis_index("zl")])
    row_tok, cols = attn.shape
    width = norm_gain.shape[0]
    top_count = expert_ids.shape[1]
    cap = 3 * row_tok // 8
    slices = owners // EXPERTS
    part = width // NEAR
    hid = w_gate.shape[1]
    slots = owners * cap
    bf16, f32 = jnp.bfloat16, jnp.float32

    copies = jnp.broadcast_to(attn[None], (n_zh, row_tok, cols))
    rows = lax.all_to_all(copies, "zh", split_axis=0, concat_axis=0, tiled=True)

    piece_type = jax.ShapeDtypeStruct((3, hid, part), bf16)
    own_gain, *pieces = pl.pallas_call(
        deal_kernel,
        in_specs=[SMEM] + [VMEM] * 4,
        out_specs=[VMEM] * (1 + NEAR),
        out_shape=[jax.ShapeDtypeStruct((1, part), f32)] + [piece_type] * NEAR,
        name="deal",
    )(place, norm_gain.reshape(1, width), w_gate[0], w_up[0], w_down[0])
    for r in range(1, NEAR):
        pieces[r] = lax.ppermute(pieces[r], QUAD, [(i, i ^ r) for i in range(NEAR)])
    rows, *pieces[1:] = lax.optimization_barrier((rows, *pieces[1:]))

    ordinal = route_ordinal(expert_ids)
    target = (expert_ids.reshape(-1) * slices) * cap + ordinal
    key = jnp.arange(slots, dtype=jnp.int32)
    key = key - ((key // cap) % slices) * cap
    hits = (target[:, None] == key[None, :]).astype(f32).reshape(row_tok, top_count, slots)
    side = (jnp.arange(2, dtype=jnp.int32)[:, None] == (jnp.arange(slots, dtype=jnp.int32) // cap) % 2).astype(f32)
    pick_rows = (jnp.sum(hits, axis=1)[None] * side[:, None]).reshape(2 * row_tok, slots).astype(bf16)
    high = (gate_fix // 256).astype(f32)
    low = (gate_fix % 256).astype(f32)
    weights = jnp.stack(
        [jnp.sum(hits * high[:, :, None], axis=1), jnp.sum(hits * low[:, :, None], axis=1)]
    )
    combine_map = (weights[:, None] * side[None, :, None]).reshape(4 * row_tok, slots).astype(bf16)

    half_zh = n_zh // 2
    rows = rows.reshape(2, half_zh, row_tok, cols).transpose(0, 2, 1, 3).reshape(2 * row_tok, part)
    outgoing = lax.dot_general(pick_rows, rows, (((0,), (0,)), ((), ())), preferred_element_type=f32)
    outgoing = outgoing.astype(bf16).reshape(owners, cap, part)
    incoming = lax.all_to_all(outgoing, EP, split_axis=0, concat_axis=0, tiled=True)

    four = NEAR * hid
    gate_up_high, gate_up_low, down = pl.pallas_call(
        gather_kernel,
        in_specs=[SMEM] + [VMEM] * (1 + NEAR),
        out_specs=[VMEM] * 3,
        out_shape=[jax.ShapeDtypeStruct((2, NEAR, hid, part), bf16)] * 2
        + [jax.ShapeDtypeStruct((NEAR, hid, part), bf16)],
        name="gather",
    )(place, own_gain, *pieces)

    group = slots // NEAR
    lanes = -(-(2 * four + 2) // LANES) * LANES
    acts = pl.pallas_call(
        act_kernel,
        grid=(NEAR,),
        in_specs=[
            pl.BlockSpec((group, part), lambda g: (g, 0)),
            pl.BlockSpec((2 * four, part), lambda g: (0, 0)),
            pl.BlockSpec((2 * four, part), lambda g: (0, 0)),
        ],
        out_specs=pl.BlockSpec((group, lanes), lambda g: (g, 0)),
        out_shape=jax.ShapeDtypeStruct((slots, lanes), bf16),
        name="acts",
    )(incoming.reshape(slots, part), gate_up_high.reshape(2 * four, part), gate_up_low.reshape(2 * four, part))
    acts = lax.all_to_all(acts.reshape(NEAR, group, lanes), QUAD, split_axis=0, concat_axis=0, tiled=True)
    sums = jnp.sum(acts.astype(f32), axis=0)
    squares = sums[:, 2 * four : 2 * four + 1] + sums[:, 2 * four + 1 : 2 * four + 2]
    inverse_rms = lax.rsqrt(squares / width + 1e-05)
    gate_act = sums[:, :four] * inverse_rms
    up_act = sums[:, four : 2 * four] * inverse_rms
    hidden_act = (jax.nn.silu(gate_act) * up_act).astype(bf16)
    spread = jnp.broadcast_to(hidden_act[None], (NEAR,) + hidden_act.shape)
    hidden_all = lax.all_to_all(spread, QUAD, split_axis=0, concat_axis=0, tiled=True)

    slice_out = jnp.dot(hidden_all.reshape(slots, four), down.reshape(four, part), preferred_element_type=f32)
    slice_out = slice_out.astype(bf16).reshape(owners, cap, part)
    returned = lax.all_to_all(slice_out, EP, split_axis=0, concat_axis=0, tiled=True)

    both = jnp.dot(combine_map, returned.reshape(slots, part), preferred_element_type=f32)
    both = both.reshape(2, 2, row_tok, half_zh, cols)
    combined = both[0] * (1.0 / 256.0) + both[1] * (1.0 / 65536.0)
    shares = combined.astype(bf16).transpose(0, 2, 1, 3).reshape(n_zh, row_tok, cols)
    shares = lax.all_to_all(shares, "zh", split_axis=0, concat_axis=0, tiled=True)
    return jnp.sum(shares.astype(f32), axis=0).astype(bf16)


def solution(mesh):
    n_ep, n_tp = mesh.devices.shape
    fine = Mesh(mesh.devices.reshape(n_ep // 4, 2, 2, n_tp // 2, 2), EP + TP)
    in_specs = (
        P(EP, TP),
        P(),
        P(EP, TP, None),
        P(EP, TP, None),
        P(EP, TP, None),
        P(EP, None),
        P(EP, None),
    )
    return jax.shard_map(body, mesh=fine, in_specs=in_specs, out_specs=P(EP, TP), check_vma=False)
```

```python
import jax
import jax.numpy as jnp
from jax import lax
from jax.experimental import pallas as pl
from jax.experimental.pallas import tpu as pltpu
from jax.sharding import Mesh
from jax.sharding import PartitionSpec as P

EXPERTS = 8
EP = ("eh", "xl", "core")
TP = ("zh", "zm", "zl")
QUAD = ("core", "zl")
NEAR = 4
SWAP = [(0, 1), (1, 0)]
LANES = 128
VMEM = pl.BlockSpec(memory_space=pltpu.VMEM)
SMEM = pl.BlockSpec(memory_space=pltpu.SMEM)


def route_ordinal(route_ids):
    flat_ids = route_ids.reshape(-1)
    onehot = (flat_ids[:, None] == jnp.arange(EXPERTS, dtype=jnp.int32)[None, :]).astype(jnp.float32)
    count = flat_ids.shape[0]
    earlier = (jnp.arange(count)[:, None] > jnp.arange(count)[None, :]).astype(jnp.float32)
    before = jnp.dot(earlier, onehot, preferred_element_type=jnp.float32)
    return jnp.sum(before * onehot, axis=1).astype(jnp.int32)


def deal_kernel(place, gain, gate, up, down, own_gain, *outs):
    blocks = gate.shape[1] // (NEAR * LANES)
    for r, out in enumerate(outs):
        core = lax.rem(place[0] + r // 2, 2)
        zl = lax.rem(place[1] + r % 2, 2)
        for i in range(blocks):
            to = slice(i * LANES, (i + 1) * LANES)
            block = i * NEAR + core * 2 + zl
            at = pl.ds(pl.multiple_of(block * LANES, LANES), LANES)
            for k, weight in enumerate((gate, up, down)):
                out[k, :, to] = weight[:, at]
            if r == 0:
                own_gain[:, to] = gain[:, at]


def gather_kernel(place, gain, *refs):
    pieces, (high, low, down) = refs[:NEAR], refs[NEAR:]
    for r, piece in enumerate(pieces):
        source = 2 * lax.rem(place[0] + r // 2, 2) + lax.rem(place[1] + r % 2, 2)
        for k in range(2):
            scaled = piece[k].astype(jnp.float32) * gain[...]
            rounded = scaled.astype(jnp.bfloat16)
            high[k, source] = rounded
            low[k, source] = (scaled - rounded.astype(jnp.float32)).astype(jnp.bfloat16)
        down[source] = piece[2]


def act_kernel(rows, high, low, out):
    x = rows[...]
    dims = (((1,), (1,)), ((), ()))
    acts = lax.dot_general(x, high[...], dims, preferred_element_type=jnp.float32)
    acts = acts + lax.dot_general(x, low[...], dims, preferred_element_type=jnp.float32)
    values = x.astype(jnp.float32)
    squares = jnp.sum(values * values, axis=1, keepdims=True)
    rounded = squares.astype(jnp.bfloat16).astype(jnp.float32)
    tail = out.shape[1] - acts.shape[1]
    column = lax.broadcasted_iota(jnp.int32, (x.shape[0], tail), 1)
    extra = jnp.where(column == 0, rounded, jnp.where(column == 1, squares - rounded, 0.0))
    out[:, : acts.shape[1]] = acts.astype(jnp.bfloat16)
    out[:, acts.shape[1] :] = extra.astype(jnp.bfloat16)


def body(attn, norm_gain, w_gate, w_up, w_down, expert_ids, gate_fix):
    owners = lax.axis_size(EP)
    n_zh = lax.axis_size("zh")
    zm = lax.axis_index("zm")
    place = jnp.stack([lax.axis_index("core"), lax.axis_index("zl")])
    row_tok, cols = attn.shape
    width = norm_gain.shape[0]
    top_count = expert_ids.shape[1]
    cap = 3 * row_tok // 8
    slices = owners // EXPERTS
    part = width // NEAR
    hid = w_gate.shape[1]
    slots = owners * cap
    bf16, f32 = jnp.bfloat16, jnp.float32

    copies = jnp.broadcast_to(attn[None], (n_zh, row_tok, cols))
    rows = lax.all_to_all(copies, "zh", split_axis=0, concat_axis=0, tiled=True)

    piece_type = jax.ShapeDtypeStruct((3, hid, part), bf16)
    own_gain, *pieces = pl.pallas_call(
        deal_kernel,
        in_specs=[SMEM] + [VMEM] * 4,
        out_specs=[VMEM] * (1 + NEAR),
        out_shape=[jax.ShapeDtypeStruct((1, part), f32)] + [piece_type] * NEAR,
        name="deal",
    )(place, norm_gain.reshape(1, width), w_gate[0], w_up[0], w_down[0])
    for r in range(1, NEAR):
        pieces[r] = lax.ppermute(pieces[r], QUAD, [(i, i ^ r) for i in range(NEAR)])

    ordinal = route_ordinal(expert_ids)
    target = (expert_ids.reshape(-1) * slices) * cap + ordinal
    key = jnp.arange(slots, dtype=jnp.int32)
    key = key - ((key // cap) % slices) * cap
    hits = (target[:, None] == key[None, :]).astype(f32).reshape(row_tok, top_count, slots)
    side = (jnp.arange(2, dtype=jnp.int32)[:, None] == (jnp.arange(slots, dtype=jnp.int32) // cap) % 2).astype(f32)
    pick_rows = (jnp.sum(hits, axis=1)[None] * side[:, None]).reshape(2 * row_tok, slots).astype(bf16)
    high = (gate_fix // 256).astype(f32)
    low = (gate_fix % 256).astype(f32)
    weights = jnp.stack(
        [jnp.sum(hits * high[:, :, None], axis=1), jnp.sum(hits * low[:, :, None], axis=1)]
    )
    combine_map = (weights[:, None] * side[None, :, None]).reshape(4 * row_tok, slots).astype(bf16)

    other = lax.ppermute(rows, "zm", SWAP)
    rows = jnp.stack([jnp.where(zm == 0, rows, other), jnp.where(zm == 0, other, rows)])
    rows = rows.transpose(0, 2, 1, 3).reshape(2 * row_tok, part)
    rows, *pieces[1:] = lax.optimization_barrier((rows, *pieces[1:]))
    outgoing = lax.dot_general(pick_rows, rows, (((0,), (0,)), ((), ())), preferred_element_type=f32)
    outgoing = outgoing.astype(bf16).reshape(owners, cap, part)
    incoming = lax.all_to_all(outgoing, EP, split_axis=0, concat_axis=0, tiled=True)

    four = NEAR * hid
    gate_up_high, gate_up_low, down = pl.pallas_call(
        gather_kernel,
        in_specs=[SMEM] + [VMEM] * (1 + NEAR),
        out_specs=[VMEM] * 3,
        out_shape=[jax.ShapeDtypeStruct((2, NEAR, hid, part), bf16)] * 2
        + [jax.ShapeDtypeStruct((NEAR, hid, part), bf16)],
        name="gather",
    )(place, own_gain, *pieces)

    group = slots // NEAR
    lanes = -(-(2 * four + 2) // LANES) * LANES
    acts = pl.pallas_call(
        act_kernel,
        grid=(NEAR,),
        in_specs=[
            pl.BlockSpec((group, part), lambda g: (g, 0)),
            pl.BlockSpec((2 * four, part), lambda g: (0, 0)),
            pl.BlockSpec((2 * four, part), lambda g: (0, 0)),
        ],
        out_specs=pl.BlockSpec((group, lanes), lambda g: (g, 0)),
        out_shape=jax.ShapeDtypeStruct((slots, lanes), bf16),
        name="acts",
    )(incoming.reshape(slots, part), gate_up_high.reshape(2 * four, part), gate_up_low.reshape(2 * four, part))
    acts = lax.all_to_all(acts.reshape(NEAR, group, lanes), QUAD, split_axis=0, concat_axis=0, tiled=True)
    sums = jnp.sum(acts.astype(f32), axis=0)
    squares = sums[:, 2 * four : 2 * four + 1] + sums[:, 2 * four + 1 : 2 * four + 2]
    inverse_rms = lax.rsqrt(squares / width + 1e-05)
    gate_act = sums[:, :four] * inverse_rms
    up_act = sums[:, four : 2 * four] * inverse_rms
    hidden_act = (jax.nn.silu(gate_act) * up_act).astype(bf16)
    spread = jnp.broadcast_to(hidden_act[None], (NEAR,) + hidden_act.shape)
    hidden_all = lax.all_to_all(spread, QUAD, split_axis=0, concat_axis=0, tiled=True)

    slice_out = jnp.dot(hidden_all.reshape(slots, four), down.reshape(four, part), preferred_element_type=f32)
    slice_out = slice_out.astype(bf16).reshape(owners, cap, part)
    returned = lax.all_to_all(slice_out, EP, split_axis=0, concat_axis=0, tiled=True)

    both = jnp.dot(combine_map, returned.reshape(slots, part), preferred_element_type=f32)
    both = both.reshape(2, 2, row_tok, part)
    combined = both[0] * (1.0 / 256.0) + both[1] * (1.0 / 65536.0)
    mine = jnp.where(zm == 0, combined[0], combined[1])
    yours = jnp.where(zm == 0, combined[1], combined[0]).astype(bf16)
    shares = mine + lax.ppermute(yours, "zm", SWAP).astype(f32)
    shares = shares.astype(bf16).reshape(row_tok, n_zh, cols).transpose(1, 0, 2)
    shares = lax.all_to_all(shares, "zh", split_axis=0, concat_axis=0, tiled=True)
    return jnp.sum(shares.astype(f32), axis=0).astype(bf16)


def solution(mesh):
    n_ep, n_tp = mesh.devices.shape
    fine = Mesh(mesh.devices.reshape(n_ep // 4, 2, 2, n_tp // 4, 2, 2), EP + TP)
    in_specs = (
        P(EP, TP),
        P(),
        P(EP, TP, None),
        P(EP, TP, None),
        P(EP, TP, None),
        P(EP, None),
        P(EP, None),
    )
    return jax.shard_map(body, mesh=fine, in_specs=in_specs, out_specs=P(EP, TP), check_vma=False)
```
